32 devices in a mesh: patch: 2 (over y), sky: 4 (over z), exp: 2 (over core), band: 2 (over x).
Axes of the slice: x: 2, y: 2, z: 4, core: 2. Of those that a mesh axis runs over, the one named last changes fastest.
Arguments:
- images: bfloat16 [2, 20, 1024, 512], P('band', 'exp', ('patch', 'sky')), parts along dimension 2, may hold values from -400 to 400
- valid_mask: int32 [2, 20, 1024, 512], P('band', 'exp', ('patch', 'sky')), parts along dimension 2, may hold values from 0 to 1, as said below
- row_kernel: float32 [2, 20, 31], P('band', 'exp'), may hold values from 0.01 to 0.06
- col_kernel: float32 [2, 20, 31], P('band', 'exp'), may hold values from 0.01 to 0.06
- exp_group: int32 [2, 20], P('band', 'exp'), may hold values from 0 to 15
- zero_point: float32 [2, 16], P('band'), may hold values from 0.5 to 2
- psf_row: float32 [2, 31], P('band'), may hold values from 0.01 to 0.06
- psf_col: float32 [2, 31], P('band'), may hold values from 0.01 to 0.06
Outputs:
- coadd_image: float32 [2, 1024, 512], P('band', ('patch', 'sky')), parts along dimension 1
- detection: float32 [1024, 512], P(('patch', 'sky'), 'band'), parts along dimension 0
The draws below stay inside these ranges and needn't reach their ends.
There are 2 independent parts, one for each index of `patch`. The reference program is written for one: setup_inputs(seed, part) draws one part's arguments, and reference() takes and returns one part's arrays. A program takes and returns all parts, laid end to end along the dimension named above; an argument that names none is the same for every part. Nothing has to cross between parts.
Inputs may be any that keep to these rules, and one draw needn't show every extreme that they name: For every band and pixel at least 10 of the 20 visits have valid_mask 1; exactly that many at some pixels, all of them at others.
All inputs are finite; a program needn't handle non-finite values.
Results may differ from the reference program's by a relative error of at most 0.0006.
Values may be sent and summed in bfloat16 or wider, within the bound.
A program may use at most 64 MiB of HBM per device.

```python
import math
import jax
import jax.numpy as jnp
from jax import lax

COLS = 512
HALF = 15
REJECT = 4
GROUPS = 16
TAPS = 31
BANDS = 2
VIS_BAND = 20
ROWS = 512


def draw_images(key, part):
    key_noise, key_col, key_spike, key_sign = jax.random.split(key, 4)
    shape_all = (BANDS, VIS_BAND, ROWS, COLS)
    row_frac = jnp.arange(ROWS, dtype=jnp.float32) / max(ROWS - 1, 1)
    col_scale = 10.0 ** (jax.random.uniform(key_col, (COLS,), jnp.float32) - 0.5)
    jitter = jax.random.normal(key_noise, shape_all, jnp.float32)
    jitter = jnp.clip(jitter, -6.0, 6.0)
    row_scale = 10.0 ** (row_frac - 0.5)
    spike_on = (jax.random.randint(key_spike, shape_all, 0, 25) == 0).astype(jnp.float32)
    spike_sign = (jax.random.randint(key_sign, shape_all, 0, 2) * 2 - 1).astype(jnp.float32)
    sampled = (jitter + 12.0 * spike_on * spike_sign) * row_scale[:, None] * col_scale[None, :]
    return sampled.astype(jnp.bfloat16)


def draw_valid_mask(key, part):
    key_score, key_limit = jax.random.split(jax.random.fold_in(key, 7), 2)
    shape_all = (BANDS, VIS_BAND, ROWS, COLS)
    scores = jax.random.randint(key_score, shape_all, 0, 1 << 20) * VIS_BAND + jnp.arange(VIS_BAND, dtype=jnp.int32)[None, :, None, None]

    def count_below(visit_num, rank_count):
        picked = lax.dynamic_index_in_dim(scores, visit_num, 1, keepdims=True)
        return rank_count + (picked < scores).astype(jnp.int32)
    rank_count = lax.fori_loop(0, VIS_BAND, count_below, jnp.zeros(shape_all, jnp.int32))
    cutoff = jax.random.randint(key_limit, (BANDS, 1, ROWS, COLS), 2 * REJECT + 2, VIS_BAND + 1)
    return (rank_count < cutoff).astype(jnp.int32)


def touch_ends(drawn, key, low, largest):
    extent = drawn.shape
    index_at = [jax.random.randint(jax.random.fold_in(key, axis), (), 0, extent[axis]) for axis in range(len(extent))]
    drawn = drawn.at[tuple(index_at)].set(low)
    longest = extent.index(max(extent))
    index_at[longest] = (index_at[longest] + 1) % extent[longest]
    return drawn.at[tuple(index_at)].set(largest)


def steps_of(key, dims, pieces, smallest, high):
    factor_of, own = 1.0, jax.random.fold_in(key, 6)
    for dim, shards_of in pieces:
        heights = jnp.exp(jax.random.uniform(jax.random.fold_in(own, dim), (shards_of,), jnp.float32, smallest / len(pieces), high / len(pieces)))
        factor_of = factor_of * jnp.repeat(heights, dims[dim] // shards_of).reshape([-1 if axis == dim else 1 for axis in range(len(dims))])
    return factor_of


def setup_inputs(seed: int = 0, part: int = 0) -> dict:
    seeds = jax.random.split(jax.random.key(seed), 9)
    own_keys = jax.random.split(jax.random.fold_in(seeds[8], part), 9)
    images = draw_images(jax.random.fold_in(jax.random.fold_in(seeds[8], part), 71), part)
    valid_mask = draw_valid_mask(jax.random.fold_in(jax.random.fold_in(seeds[8], part), 71), part)
    row_kernel = jnp.clip(jnp.exp(math.log(0.06) - 1.7917595 * jax.random.uniform(seeds[2], (BANDS, VIS_BAND, TAPS), jnp.float32) ** steps_of(seeds[2], (BANDS, VIS_BAND, TAPS), ((0, 2), (1, 2)), -0.2, 0.2)), 0.01, 0.06)
    col_kernel = jnp.clip(jnp.exp(math.log(0.06) - 1.7917595 * jax.random.uniform(seeds[3], (BANDS, VIS_BAND, TAPS), jnp.float32) ** steps_of(seeds[3], (BANDS, VIS_BAND, TAPS), ((0, 2), (1, 2)), -0.2, 0.2)), 0.01, 0.06)
    exp_group = touch_ends(jax.random.randint(seeds[4], (BANDS, VIS_BAND), 0, GROUPS), jax.random.fold_in(seeds[4], 1), 0, GROUPS - 1).astype(jnp.int32)
    zero_point = jnp.clip(jnp.exp(math.log(2.0) - 1.3862944 * jax.random.uniform(seeds[5], (BANDS, GROUPS), jnp.float32) ** steps_of(seeds[5], (BANDS, GROUPS), ((0, 2),), -0.2, 0.2)), 0.5, 2.0)
    psf_row = jnp.clip(jnp.exp(math.log(0.06) - 1.7917595 * jax.random.uniform(seeds[6], (BANDS, TAPS), jnp.float32) ** steps_of(seeds[6], (BANDS, TAPS), ((0, 2),), -0.2, 0.2)), 0.01, 0.06)
    psf_col = jnp.clip(jnp.exp(math.log(0.06) - 1.7917595 * jax.random.uniform(seeds[7], (BANDS, TAPS), jnp.float32) ** steps_of(seeds[7], (BANDS, TAPS), ((0, 2),), -0.2, 0.2)), 0.01, 0.06)
    return dict(images=images, valid_mask=valid_mask, row_kernel=row_kernel, col_kernel=col_kernel, exp_group=exp_group, zero_point=zero_point, psf_row=psf_row, psf_col=psf_col)


SENTINEL = 1.0e30
EPSILON = 1.0e-5


def rows_filter(padded, kernel, height):
    result = kernel[..., 0][..., None, None] * padded[..., 0:height, :]
    for offset in range(1, TAPS):
        result = result + kernel[..., offset][..., None, None] * padded[..., offset:offset + height, :]
    return result


def cols_filter(grid_in, kernel):
    columns = grid_in.shape[-1]
    widths = [(0, 0)] * (grid_in.ndim - 1) + [(HALF, HALF)]
    padded = jnp.pad(grid_in, widths)
    result = kernel[..., 0][..., None, None] * padded[..., 0:columns]
    for offset in range(1, TAPS):
        result = result + kernel[..., offset][..., None, None] * padded[..., offset:offset + columns]
    return result


def one_band(inputs):
    band_images, band_valid, band_rows, band_cols, band_groups, band_points = inputs
    padded = jnp.pad(band_images.astype(jnp.float32), ((0, 0), (HALF, HALF), (0, 0)))
    smeared = cols_filter(rows_filter(padded, band_rows, ROWS), band_cols)
    matches = band_groups[:, None] == jnp.arange(GROUPS, dtype=jnp.int32)[None, :]
    flux_scale = jnp.sum(jnp.where(matches, band_points[None, :], jnp.float32(0.0)), axis=1)
    scaled_visits = flux_scale[:, None, None] * smeared
    usable = band_valid == 1
    upper_sum = jnp.sum(jnp.sort(jnp.where(usable, scaled_visits, -SENTINEL), axis=0)[VIS_BAND - REJECT:], axis=0)
    lower_sum = jnp.sum(jnp.sort(jnp.where(usable, scaled_visits, SENTINEL), axis=0)[:REJECT], axis=0)
    flux_sum = jnp.sum(jnp.where(usable, scaled_visits, jnp.float32(0.0)), axis=0)
    valid_count = jnp.sum(usable.astype(jnp.float32), axis=0)
    return (flux_sum - upper_sum - lower_sum) / (valid_count - 2 * REJECT)


def reference(images, valid_mask, row_kernel, col_kernel, exp_group, zero_point, psf_row, psf_col):
    coadd_image = lax.map(one_band, (images, valid_mask, row_kernel, col_kernel, exp_group, zero_point))
    padded = jnp.pad(coadd_image, ((0, 0), (HALF, HALF), (0, 0)))
    filtered = cols_filter(rows_filter(padded, psf_row, ROWS), psf_col)
    energy = filtered * filtered
    variance = jnp.sum(energy, axis=(1, 2)) / (ROWS * COLS) + EPSILON
    detection = jnp.sum(energy / variance[:, None, None], axis=0)
    return (coadd_image, detection)
```

```python
import functools

import jax
import jax.numpy as jnp
from jax import lax
from jax.experimental import pallas as pl
from jax.experimental.pallas import tpu as pltpu
from jax.sharding import PartitionSpec as P

MESH = pl.DeviceIdType.MESH
HALF = 15
REJECT = 4
TAPS = 31
SENTINEL = 1e30
EPSILON = 1e-05
PAD = 16
TILE = 128
CHUNKS = 4
BF = jnp.bfloat16
F32 = jnp.float32


def parts(value):
    high = value.astype(BF)
    return high, (value - high.astype(F32)).astype(BF)


def mm(a, b):
    return jnp.dot(a, b, preferred_element_type=F32)


def cols_filter(high, low, wh_ref, wl_ref):
    columns = high.shape[1]
    outs = []
    for start in range(0, columns, 2 * TILE):
        lo_in, hi_in = max(start - TILE, 0), min(start + 3 * TILE, columns)
        base = lo_in - (start - TILE)
        span = pl.ds(base, hi_in - lo_in)
        wh, wl = wh_ref[span, :], wl_ref[span, :]
        h, l = high[:, lo_in:hi_in], low[:, lo_in:hi_in]
        outs.append(mm(h, wh) + mm(l, wh) + mm(h, wl))
    return outs


def insert(ordered, incoming, first, second):
    updated = []
    for held in ordered:
        updated.append(first(held, incoming))
        incoming = second(held, incoming)
    if len(updated) < REJECT:
        updated.append(incoming)
    return updated


def kernel(
    n_sky, n_band,
    img, mask, rk, ck, pr, pc, eg, zp,
    coadd_out, det_out,
    x, msk, taps_r, taps_c, trow, wh, wl, vals, lists, other, cpad, energy, peer_energy, sums, det,
    img_sem, mask_sem, halo_send, halo_recv, list_send, list_recv, co_send, co_recv, sum_send, sum_recv,
    en_send, en_recv, out_sem,
):
    visits, height, columns = img.shape[1:]
    width = columns // n_band
    crows = height // CHUNKS
    sky, band, exp = lax.axis_index("sky"), lax.axis_index("band"), lax.axis_index("exp")
    has_before, has_after = sky > 0, sky < n_sky - 1
    n_peer = n_sky * n_band
    me = sky * n_band + band

    load_img = pltpu.make_async_copy(img.at[0], x.at[:, pl.ds(PAD, height), :], img_sem)
    load_img.start()
    load_mask = pltpu.make_async_copy(mask.at[0], msk, mask_sem)
    load_mask.start()

    def peer_of(step):
        peer = lax.rem(me + step, n_peer)
        return {"sky": peer // n_band, "band": lax.rem(peer, n_band)}

    barrier = pltpu.get_barrier_semaphore()
    for step in range(1, n_peer):
        pl.semaphore_signal(barrier, inc=1, device_id=peer_of(step), device_id_type=MESH)
    pl.semaphore_signal(barrier, inc=1, device_id={"exp": 1 - exp}, device_id_type=MESH)

    taps_r[...] = jnp.zeros_like(taps_r)
    taps_c[...] = jnp.zeros_like(taps_c)
    taps_r[0:visits, 0:TAPS] = rk[0]
    taps_r[visits:visits + 1, 0:TAPS] = pr[...]
    for v in range(visits):
        taps_c[v:v + 1, 0:TAPS] = ck[0, v:v + 1] * zp[0, eg[0, v]]
    taps_c[visits:visits + 1, 0:TAPS] = pc[...]
    at_row = lax.broadcasted_iota(jnp.int32, (TILE, TILE), 0)
    at_col = lax.broadcasted_iota(jnp.int32, (TILE, TILE), 1)
    flip = (at_col == lax.rem(HALF - at_row + TILE, TILE)).astype(F32)
    taps_c[...] = jnp.dot(taps_c[...], flip, preferred_element_type=F32, precision=lax.Precision.HIGHEST)

    def build(v, carry):
        band_r = jnp.broadcast_to(taps_r[pl.ds(v, 1), :], (TILE, TILE))
        band_r = pltpu.roll(band_r, 1, 1, stride=1, stride_axis=0)
        high, low = parts(jnp.where(at_col >= at_row, band_r, 0.0))
        trow[v, 0:TILE, 0:TILE] = high
        trow[v, TILE:2 * TILE, 0:TILE] = low
        high, low = parts(jnp.where(at_col < at_row, band_r, 0.0))
        trow[v, 0:TILE, TILE:2 * TILE] = high
        trow[v, TILE:2 * TILE, TILE:2 * TILE] = low
        band_c = jnp.broadcast_to(taps_c[pl.ds(v, 1), :], (TILE, TILE))
        band_c = pltpu.roll(band_c, 0, 1, stride=1, stride_axis=0)
        before = at_row - at_col > TILE // 2
        after = at_col - at_row > TILE // 2
        zero = jnp.zeros((TILE, TILE), BF)
        for half, ref in enumerate((wh, wl)):
            b_prev = parts(jnp.where(before, band_c, 0.0))[half]
            b_next = parts(jnp.where(after, band_c, 0.0))[half]
            b_here = parts(jnp.where(before | after, 0.0, band_c))[half]
            for k, row in enumerate(((b_prev, zero), (b_here, b_prev), (b_next, b_here), (zero, b_next))):
                for n, block in enumerate(row):
                    ref[v, k * TILE:(k + 1) * TILE, n * TILE:(n + 1) * TILE] = block
        return carry

    lax.fori_loop(0, visits + 1, build, 0)
    pl.semaphore_wait(barrier, n_peer)

    def halo(v, side):
        start, land = ((height - PAD, 0), (0, PAD + height))[side]
        return pltpu.make_async_remote_copy(
            src_ref=img.at[0, v, pl.ds(start, PAD), :],
            dst_ref=x.at[v, pl.ds(land, PAD), :],
            send_sem=halo_send.at[side, v], recv_sem=halo_recv.at[side, v],
            device_id={"sky": lax.rem(sky + (1, n_sky - 1)[side], n_sky)}, device_id_type=MESH,
        )

    def start_halo(v, carry):
        @pl.when(has_after)
        def _():
            halo(v, 0).start()

        @pl.when(has_before)
        def _():
            halo(v, 1).start()
        return carry

    lax.fori_loop(0, visits, start_halo, 0)

    @pl.when(jnp.logical_not(has_before))
    def _():
        x[:, 0:PAD, :] = jnp.zeros((visits, PAD, columns), BF)
        cpad[0:PAD, :] = jnp.zeros((PAD, columns), F32)

    @pl.when(jnp.logical_not(has_after))
    def _():
        x[:, PAD + height:, :] = jnp.zeros((visits, PAD, columns), BF)
        cpad[PAD + height:, :] = jnp.zeros((PAD, columns), F32)

    load_img.wait()
    tall = height + 2 * PAD

    def convolve(v, carry):
        @pl.when(has_before)
        def _():
            halo(v, 0).wait_recv()

        @pl.when(has_after)
        def _():
            halo(v, 1).wait_recv()
        smeared = mm(trow[v, :, 0:tall], x[v])
        high, low = parts(smeared[0:height] + smeared[height:])
        for n, block in enumerate(cols_filter(high, low, wh.at[v], wl.at[v])):
            vals[v, :, n * 2 * TILE:(n + 1) * 2 * TILE] = block
        return carry

    lax.fori_loop(0, visits, convolve, 0)
    load_mask.wait()

    def exchange(c):
        return pltpu.make_async_remote_copy(
            src_ref=lists.at[c], dst_ref=other.at[c], send_sem=list_send.at[c], recv_sem=list_recv.at[c],
            device_id={"exp": 1 - exp}, device_id_type=MESH,
        )

    def select(c, carry):
        def group(g, inner):
            rows = pl.ds(pl.multiple_of(c * crows + g * 8, 8), 8)
            upper, lower, total, count = [], [], None, None
            for v in range(visits):
                value, used = vals[v, rows, :], msk[v, rows, :]
                live = used == 1
                upper = insert(upper, jnp.where(live, value, -SENTINEL), jnp.maximum, jnp.minimum)
                lower = insert(lower, jnp.where(live, value, SENTINEL), jnp.minimum, jnp.maximum)
                kept = jnp.where(live, value, 0.0)
                total = kept if total is None else total + kept
                count = used if count is None else count + used
            spot = pl.ds(pl.multiple_of(g * 8, 8), 8)
            for k, item in enumerate(upper + lower + [total, count.astype(F32)]):
                lists[c, k, spot, :] = item
            return inner

        lax.fori_loop(0, crows // 8, group, 0)
        exchange(c).start()
        return carry

    lax.fori_loop(0, CHUNKS, select, 0)

    def merge(c, carry):
        exchange(c).wait_recv()

        def group(g, inner):
            spot = pl.ds(pl.multiple_of(g * 8, 8), 8)
            own = [lists[c, k, spot, :] for k in range(2 * REJECT + 2)]
            far = [other[c, k, spot, :] for k in range(2 * REJECT + 2)]
            ends = [jnp.maximum(own[k], far[REJECT - 1 - k]) for k in range(REJECT)]
            ends += [jnp.minimum(own[REJECT + k], far[2 * REJECT - 1 - k]) for k in range(REJECT)]
            upper_sum = (ends[0] + ends[1]) + (ends[2] + ends[3])
            lower_sum = (ends[4] + ends[5]) + (ends[6] + ends[7])
            flux, count = own[8] + far[8], own[9] + far[9]
            rows = pl.ds(pl.multiple_of(PAD + c * crows + g * 8, 8), 8)
            cpad[rows, :] = (flux - upper_sum - lower_sum) / (count - 2 * REJECT)
            return inner

        lax.fori_loop(0, crows // 8, group, 0)
        return carry

    lax.fori_loop(0, CHUNKS, merge, 0)

    def co_halo(side):
        start, land = ((height, 0), (PAD, PAD + height))[side]
        return pltpu.make_async_remote_copy(
            src_ref=cpad.at[pl.ds(start, PAD), :], dst_ref=cpad.at[pl.ds(land, PAD), :],
            send_sem=co_send.at[side], recv_sem=co_recv.at[side],
            device_id={"sky": lax.rem(sky + (1, n_sky - 1)[side], n_sky)}, device_id_type=MESH,
        )

    store_coadd = pltpu.make_async_copy(cpad.at[pl.ds(PAD, height), :], coadd_out.at[0], out_sem.at[0])

    @pl.when(has_after)
    def _():
        co_halo(0).start()

    @pl.when(has_before)
    def _():
        co_halo(1).start()
    store_coadd.start()

    @pl.when(has_before)
    def _():
        co_halo(0).wait_recv()

    @pl.when(has_after)
    def _():
        co_halo(1).wait_recv()
    high, low = parts(cpad[...])
    both = mm(trow[visits, :, 0:tall], high)
    smeared = both[0:height] + both[height:] + mm(trow[visits, 0:height, 0:tall], low)
    high, low = parts(smeared)
    partial = jnp.zeros((8, TILE), F32)
    for n, block in enumerate(cols_filter(high, low, wh.at[visits], wl.at[visits])):
        squared = block * block
        energy[:, n * 2 * TILE:(n + 1) * 2 * TILE] = squared
        for r in range(0, height, 8):
            for q in range(0, 2 * TILE, TILE):
                partial = partial + squared[r:r + 8, q:q + TILE]
    sums[pl.ds(me, 1)] = partial[None]

    def send_sum(step):
        return pltpu.make_async_remote_copy(
            src_ref=sums.at[me], dst_ref=sums.at[me], send_sem=sum_send.at[step - 1], recv_sem=sum_recv.at[step - 1],
            device_id=peer_of(step), device_id_type=MESH,
        )

    def send_energy(step):
        target = lax.rem(band + step, n_band)
        return pltpu.make_async_remote_copy(
            src_ref=energy.at[:, pl.ds(pl.multiple_of(target * width, TILE), width)],
            dst_ref=peer_energy.at[step - 1],
            send_sem=en_send.at[step - 1], recv_sem=en_recv.at[step - 1],
            device_id={"band": target}, device_id_type=MESH,
        )

    for step in range(1, n_peer):
        send_sum(step).start()
    for step in range(1, n_band):
        send_energy(step).start()
    for step in range(1, n_peer):
        send_sum(step).wait_recv()

    pixels = height * n_sky * columns

    def inverse(source):
        total = sums[source]
        for s in range(1, n_sky):
            total = total + sums[source + s * n_band]
        return 1.0 / (jnp.sum(total, keepdims=True) / pixels + EPSILON)

    mine = pl.ds(pl.multiple_of(band * width, TILE), width)
    total = energy[:, mine] * inverse(band)
    for step in range(1, n_band):
        send_energy(step).wait_recv()
        total = total + peer_energy[step - 1] * inverse(lax.rem(band + n_band - step, n_band))
    det[...] = total
    store_det = pltpu.make_async_copy(det, det_out, out_sem.at[1])
    store_det.start()

    def drain(v, carry):
        @pl.when(has_after)
        def _():
            halo(v, 0).wait_send()

        @pl.when(has_before)
        def _():
            halo(v, 1).wait_send()
        return carry

    lax.fori_loop(0, visits, drain, 0)

    @pl.when(has_after)
    def _():
        co_halo(0).wait_send()

    @pl.when(has_before)
    def _():
        co_halo(1).wait_send()
    for c in range(CHUNKS):
        exchange(c).wait_send()
    for step in range(1, n_peer):
        send_sum(step).wait_send()
    for step in range(1, n_band):
        send_energy(step).wait_send()
    store_coadd.wait()
    store_det.wait()


def solution(mesh):
    n_sky, n_band = mesh.shape["sky"], mesh.shape["band"]

    def on_device(images, valid_mask, row_kernel, col_kernel, exp_group, zero_point, psf_row, psf_col):
        _, visits, height, columns = images.shape
        assert height == TILE and mesh.shape["exp"] == 2 and visits >= REJECT
        width = columns // n_band
        tall = height + 2 * PAD
        n_list = 2 * REJECT + 2
        crows = height // CHUNKS
        kernels = visits + 1
        table = -(-kernels // 8) * 8
        vmem, smem, hbm = (
            pl.BlockSpec(memory_space=space) for space in (pltpu.VMEM, pltpu.SMEM, pl.ANY)
        )
        dma = pltpu.SemaphoreType.DMA
        return pl.pallas_call(
            functools.partial(kernel, n_sky, n_band),
            out_shape=(
                jax.ShapeDtypeStruct((1, height, columns), F32),
                jax.ShapeDtypeStruct((height, width), F32),
            ),
            in_specs=[hbm, hbm, vmem, vmem, vmem, vmem, smem, smem],
            out_specs=(hbm, hbm),
            scratch_shapes=[
                pltpu.VMEM((visits, tall, columns), BF),
                pltpu.VMEM((visits, height, columns), jnp.int32),
                pltpu.VMEM((table, TILE), F32),
                pltpu.VMEM((table, TILE), F32),
                pltpu.VMEM((kernels, 2 * TILE, 2 * TILE), BF),
                pltpu.VMEM((kernels, 4 * TILE, 2 * TILE), BF),
                pltpu.VMEM((kernels, 4 * TILE, 2 * TILE), BF),
                pltpu.VMEM((visits, height, columns), F32),
                pltpu.VMEM((CHUNKS, n_list, crows, columns), F32),
                pltpu.VMEM((CHUNKS, n_list, crows, columns), F32),
                pltpu.VMEM((tall, columns), F32),
                pltpu.VMEM((height, columns), F32),
                pltpu.VMEM((n_band - 1, height, width), F32),
                pltpu.VMEM((n_sky * n_band, 8, TILE), F32),
                pltpu.VMEM((height, width), F32),
                dma, dma, dma((2, visits)), dma((2, visits)), dma((CHUNKS,)), dma((CHUNKS,)),
                dma((2,)), dma((2,)), dma((n_sky * n_band - 1,)), dma((n_sky * n_band - 1,)), dma((n_band - 1,)), dma((n_band - 1,)), dma((2,)),
            ],
            compiler_params=pltpu.CompilerParams(
                collective_id=0, has_side_effects=True, vmem_limit_bytes=48 * 1024 * 1024
            ),
        )(images, valid_mask, row_kernel, col_kernel, psf_row, psf_col, exp_group, zero_point)

    placed = (
        P("band", "exp", ("patch", "sky"), None),
        P("band", "exp", ("patch", "sky"), None),
        P("band", "exp", None),
        P("band", "exp", None),
        P("band", "exp"),
        P("band", None),
        P("band", None),
        P("band", None),
    )
    return jax.shard_map(
        on_device,
        mesh=mesh,
        in_specs=placed,
        out_specs=(P("band", ("patch", "sky"), None), P(("patch", "sky"), "band")),
        check_vma=False,
    )
```

```python
import functools

import jax
import jax.numpy as jnp
from jax import lax
from jax.experimental import pallas as pl
from jax.experimental.pallas import tpu as pltpu
from jax.sharding import PartitionSpec as P

MESH = pl.DeviceIdType.MESH
HALF = 15
REJECT = 4
TAPS = 31
SENTINEL = 1e30
EPSILON = 1e-05
PAD = 16
TILE = 128
CHUNKS = 4
BF = jnp.bfloat16
F32 = jnp.float32


def parts(value):
    high = value.astype(BF)
    return high, (value - high.astype(F32)).astype(BF)


def mm(a, b):
    return jnp.dot(a, b, preferred_element_type=F32)


def cols_filter(high, low, wh_ref, wl_ref):
    columns = high.shape[1]
    outs = []
    for start in range(0, columns, 2 * TILE):
        lo_in, hi_in = max(start - TILE, 0), min(start + 3 * TILE, columns)
        base = lo_in - (start - TILE)
        span = pl.ds(base, hi_in - lo_in)
        wh, wl = wh_ref[span, :], wl_ref[span, :]
        h, l = high[:, lo_in:hi_in], low[:, lo_in:hi_in]
        outs.append(mm(h, wh) + mm(l, wh) + mm(h, wl))
    return outs


def insert(ordered, incoming, first, second):
    updated = []
    for held in ordered:
        updated.append(first(held, incoming))
        incoming = second(held, incoming)
    if len(updated) < REJECT:
        updated.append(incoming)
    return updated


def kernel(
    n_sky, n_band,
    img, mask, rk_in, ck_in, pr_in, pc_in, eg_in, zp_in,
    coadd_out, det_out,
    rk, ck, pr, pc, eg, zp, x, msk, taps_r, taps_c, trow, wh, wl, vals, lists, other, cpad, energy, peer_energy, sums, det,
    arg_sem, img_sem, mask_sem, halo_send, halo_recv, list_send, list_recv, co_send, co_recv, sum_send, sum_recv,
    en_send, en_recv, out_sem,
):
    visits, height, columns = img.shape[1:]
    width = columns // n_band
    crows = height // CHUNKS
    sky, band, exp = lax.axis_index("sky"), lax.axis_index("band"), lax.axis_index("exp")
    has_before, has_after = sky > 0, sky < n_sky - 1
    n_peer = n_sky * n_band
    me = sky * n_band + band

    small = [
        pltpu.make_async_copy(source, target, arg_sem.at[k])
        for k, (source, target) in enumerate(
            ((eg_in, eg), (zp_in, zp), (ck_in, ck), (pc_in, pc), (rk_in, rk), (pr_in, pr))
        )
    ]
    for copy in small:
        copy.start()
    load_img = pltpu.make_async_copy(img.at[0], x.at[:, pl.ds(PAD, height), :], img_sem)
    load_img.start()
    load_mask = pltpu.make_async_copy(mask.at[0], msk, mask_sem)
    load_mask.start()

    def peer_of(step):
        peer = lax.rem(me + step, n_peer)
        return {"sky": peer // n_band, "band": lax.rem(peer, n_band)}

    barrier = pltpu.get_barrier_semaphore()
    for step in range(1, n_peer):
        pl.semaphore_signal(barrier, inc=1, device_id=peer_of(step), device_id_type=MESH)
    pl.semaphore_signal(barrier, inc=1, device_id={"exp": 1 - exp}, device_id_type=MESH)

    taps_r[...] = jnp.zeros_like(taps_r)
    taps_c[...] = jnp.zeros_like(taps_c)
    for copy in small:
        copy.wait()
    for v in range(visits):
        taps_r[v:v + 1, 0:TAPS] = rk[v]
    taps_r[visits:visits + 1, 0:TAPS] = pr[...]
    for v in range(visits):
        taps_c[v:v + 1, 0:TAPS] = ck[v] * zp[0, eg[0, v]]
    taps_c[visits:visits + 1, 0:TAPS] = pc[...]
    at_row = lax.broadcasted_iota(jnp.int32, (TILE, TILE), 0)
    at_col = lax.broadcasted_iota(jnp.int32, (TILE, TILE), 1)
    flip = (at_col == lax.rem(HALF - at_row + TILE, TILE)).astype(F32)
    taps_c[...] = jnp.dot(taps_c[...], flip, preferred_element_type=F32, precision=lax.Precision.HIGHEST)

    def build(v, carry):
        band_r = jnp.broadcast_to(taps_r[pl.ds(v, 1), :], (TILE, TILE))
        band_r = pltpu.roll(band_r, 1, 1, stride=1, stride_axis=0)
        high, low = parts(jnp.where(at_col >= at_row, band_r, 0.0))
        trow[v, 0:TILE, 0:TILE] = high
        trow[v, TILE:2 * TILE, 0:TILE] = low
        high, low = parts(jnp.where(at_col < at_row, band_r, 0.0))
        trow[v, 0:TILE, TILE:2 * TILE] = high
        trow[v, TILE:2 * TILE, TILE:2 * TILE] = low
        band_c = jnp.broadcast_to(taps_c[pl.ds(v, 1), :], (TILE, TILE))
        band_c = pltpu.roll(band_c, 0, 1, stride=1, stride_axis=0)
        before = at_row - at_col > TILE // 2
        after = at_col - at_row > TILE // 2
        zero = jnp.zeros((TILE, TILE), BF)
        for half, ref in enumerate((wh, wl)):
            b_prev = parts(jnp.where(before, band_c, 0.0))[half]
            b_next = parts(jnp.where(after, band_c, 0.0))[half]
            b_here = parts(jnp.where(before | after, 0.0, band_c))[half]
            for k, row in enumerate(((b_prev, zero), (b_here, b_prev), (b_next, b_here), (zero, b_next))):
                for n, block in enumerate(row):
                    ref[v, k * TILE:(k + 1) * TILE, n * TILE:(n + 1) * TILE] = block
        return carry

    lax.fori_loop(0, visits + 1, build, 0)
    pl.semaphore_wait(barrier, n_peer)

    def halo(v, side):
        start, land = ((height - PAD, 0), (0, PAD + height))[side]
        return pltpu.make_async_remote_copy(
            src_ref=img.at[0, v, pl.ds(start, PAD), :],
            dst_ref=x.at[v, pl.ds(land, PAD), :],
            send_sem=halo_send.at[side, v], recv_sem=halo_recv.at[side, v],
            device_id={"sky": lax.rem(sky + (1, n_sky - 1)[side], n_sky)}, device_id_type=MESH,
        )

    def start_halo(v, carry):
        @pl.when(has_after)
        def _():
            halo(v, 0).start()

        @pl.when(has_before)
        def _():
            halo(v, 1).start()
        return carry

    lax.fori_loop(0, visits, start_halo, 0)

    @pl.when(jnp.logical_not(has_before))
    def _():
        x[:, 0:PAD, :] = jnp.zeros((visits, PAD, columns), BF)
        cpad[0:PAD, :] = jnp.zeros((PAD, columns), F32)

    @pl.when(jnp.logical_not(has_after))
    def _():
        x[:, PAD + height:, :] = jnp.zeros((visits, PAD, columns), BF)
        cpad[PAD + height:, :] = jnp.zeros((PAD, columns), F32)

    load_img.wait()
    tall = height + 2 * PAD

    def convolve(v, carry):
        @pl.when(has_before)
        def _():
            halo(v, 0).wait_recv()

        @pl.when(has_after)
        def _():
            halo(v, 1).wait_recv()
        smeared = mm(trow[v, :, 0:tall], x[v])
        high, low = parts(smeared[0:height] + smeared[height:])
        for n, block in enumerate(cols_filter(high, low, wh.at[v], wl.at[v])):
            vals[v, :, n * 2 * TILE:(n + 1) * 2 * TILE] = block
        return carry

    lax.fori_loop(0, visits, convolve, 0)
    load_mask.wait()

    def exchange(c):
        return pltpu.make_async_remote_copy(
            src_ref=lists.at[c], dst_ref=other.at[c], send_sem=list_send.at[c], recv_sem=list_recv.at[c],
            device_id={"exp": 1 - exp}, device_id_type=MESH,
        )

    def select(c, carry):
        def group(g, inner):
            rows = pl.ds(pl.multiple_of(c * crows + g * 8, 8), 8)
            upper, lower, total, count = [], [], None, None
            for v in range(visits):
                value, used = vals[v, rows, :], msk[v, rows, :]
                live = used == 1
                upper = insert(upper, jnp.where(live, value, -SENTINEL), jnp.maximum, jnp.minimum)
                lower = insert(lower, jnp.where(live, value, SENTINEL), jnp.minimum, jnp.maximum)
                kept = jnp.where(live, value, 0.0)
                total = kept if total is None else total + kept
                count = used if count is None else count + used
            spot = pl.ds(pl.multiple_of(g * 8, 8), 8)
            for k, item in enumerate(upper + lower + [total, count.astype(F32)]):
                lists[c, k, spot, :] = item
            return inner

        lax.fori_loop(0, crows // 8, group, 0)
        exchange(c).start()
        return carry

    lax.fori_loop(0, CHUNKS, select, 0)

    def merge(c, carry):
        exchange(c).wait_recv()

        def group(g, inner):
            spot = pl.ds(pl.multiple_of(g * 8, 8), 8)
            own = [lists[c, k, spot, :] for k in range(2 * REJECT + 2)]
            far = [other[c, k, spot, :] for k in range(2 * REJECT + 2)]
            ends = [jnp.maximum(own[k], far[REJECT - 1 - k]) for k in range(REJECT)]
            ends += [jnp.minimum(own[REJECT + k], far[2 * REJECT - 1 - k]) for k in range(REJECT)]
            upper_sum = (ends[0] + ends[1]) + (ends[2] + ends[3])
            lower_sum = (ends[4] + ends[5]) + (ends[6] + ends[7])
            flux, count = own[8] + far[8], own[9] + far[9]
            rows = pl.ds(pl.multiple_of(PAD + c * crows + g * 8, 8), 8)
            cpad[rows, :] = (flux - upper_sum - lower_sum) / (count - 2 * REJECT)
            return inner

        lax.fori_loop(0, crows // 8, group, 0)
        return carry

    lax.fori_loop(0, CHUNKS, merge, 0)

    def co_halo(side):
        start, land = ((height, 0), (PAD, PAD + height))[side]
        return pltpu.make_async_remote_copy(
            src_ref=cpad.at[pl.ds(start, PAD), :], dst_ref=cpad.at[pl.ds(land, PAD), :],
            send_sem=co_send.at[side], recv_sem=co_recv.at[side],
            device_id={"sky": lax.rem(sky + (1, n_sky - 1)[side], n_sky)}, device_id_type=MESH,
        )

    store_coadd = pltpu.make_async_copy(cpad.at[pl.ds(PAD, height), :], coadd_out.at[0], out_sem.at[0])

    @pl.when(has_after)
    def _():
        co_halo(0).start()

    @pl.when(has_before)
    def _():
        co_halo(1).start()
    store_coadd.start()

    @pl.when(has_before)
    def _():
        co_halo(0).wait_recv()

    @pl.when(has_after)
    def _():
        co_halo(1).wait_recv()
    high, low = parts(cpad[...])
    both = mm(trow[visits, :, 0:tall], high)
    smeared = both[0:height] + both[height:] + mm(trow[visits, 0:height, 0:tall], low)
    high, low = parts(smeared)
    partial = jnp.zeros((8, TILE), F32)
    for n, block in enumerate(cols_filter(high, low, wh.at[visits], wl.at[visits])):
        squared = block * block
        energy[:, n * 2 * TILE:(n + 1) * 2 * TILE] = squared
        for r in range(0, height, 8):
            for q in range(0, 2 * TILE, TILE):
                partial = partial + squared[r:r + 8, q:q + TILE]
    sums[pl.ds(me, 1)] = partial[None]

    def send_sum(step):
        return pltpu.make_async_remote_copy(
            src_ref=sums.at[me], dst_ref=sums.at[me], send_sem=sum_send.at[step - 1], recv_sem=sum_recv.at[step - 1],
            device_id=peer_of(step), device_id_type=MESH,
        )

    def send_energy(step):
        target = lax.rem(band + step, n_band)
        return pltpu.make_async_remote_copy(
            src_ref=energy.at[:, pl.ds(pl.multiple_of(target * width, TILE), width)],
            dst_ref=peer_energy.at[step - 1],
            send_sem=en_send.at[step - 1], recv_sem=en_recv.at[step - 1],
            device_id={"band": target}, device_id_type=MESH,
        )

    for step in range(1, n_peer):
        send_sum(step).start()
    for step in range(1, n_band):
        send_energy(step).start()
    for step in range(1, n_peer):
        send_sum(step).wait_recv()

    pixels = height * n_sky * columns

    def inverse(source):
        total = sums[source]
        for s in range(1, n_sky):
            total = total + sums[source + s * n_band]
        return 1.0 / (jnp.sum(total, keepdims=True) / pixels + EPSILON)

    mine = pl.ds(pl.multiple_of(band * width, TILE), width)
    total = energy[:, mine] * inverse(band)
    for step in range(1, n_band):
        send_energy(step).wait_recv()
        total = total + peer_energy[step - 1] * inverse(lax.rem(band + n_band - step, n_band))
    det[...] = total
    store_det = pltpu.make_async_copy(det, det_out, out_sem.at[1])
    store_det.start()

    def drain(v, carry):
        @pl.when(has_after)
        def _():
            halo(v, 0).wait_send()

        @pl.when(has_before)
        def _():
            halo(v, 1).wait_send()
        return carry

    lax.fori_loop(0, visits, drain, 0)

    @pl.when(has_after)
    def _():
        co_halo(0).wait_send()

    @pl.when(has_before)
    def _():
        co_halo(1).wait_send()
    for c in range(CHUNKS):
        exchange(c).wait_send()
    for step in range(1, n_peer):
        send_sum(step).wait_send()
    for step in range(1, n_band):
        send_energy(step).wait_send()
    store_coadd.wait()
    store_det.wait()


def solution(mesh):
    n_sky, n_band = mesh.shape["sky"], mesh.shape["band"]

    def on_device(images, valid_mask, row_kernel, col_kernel, exp_group, zero_point, psf_row, psf_col):
        _, visits, height, columns = images.shape
        assert height == TILE and mesh.shape["exp"] == 2 and visits >= REJECT
        width = columns // n_band
        tall = height + 2 * PAD
        n_list = 2 * REJECT + 2
        crows = height // CHUNKS
        kernels = visits + 1
        table = -(-kernels // 8) * 8
        hbm, anywhere = (pl.BlockSpec(memory_space=space) for space in (pltpu.HBM, pl.ANY))
        dma = pltpu.SemaphoreType.DMA
        return pl.pallas_call(
            functools.partial(kernel, n_sky, n_band),
            out_shape=(
                jax.ShapeDtypeStruct((1, height, columns), F32),
                jax.ShapeDtypeStruct((height, width), F32),
            ),
            in_specs=[hbm] * 8,
            out_specs=(anywhere, anywhere),
            scratch_shapes=[
                pltpu.VMEM((visits, 1, TAPS), F32),
                pltpu.VMEM((visits, 1, TAPS), F32),
                pltpu.VMEM((1, TAPS), F32),
                pltpu.VMEM((1, TAPS), F32),
                pltpu.SMEM(exp_group.shape, jnp.int32),
                pltpu.SMEM(zero_point.shape, F32),
                pltpu.VMEM((visits, tall, columns), BF),
                pltpu.VMEM((visits, height, columns), jnp.int32),
                pltpu.VMEM((table, TILE), F32),
                pltpu.VMEM((table, TILE), F32),
                pltpu.VMEM((kernels, 2 * TILE, 2 * TILE), BF),
                pltpu.VMEM((kernels, 4 * TILE, 2 * TILE), BF),
                pltpu.VMEM((kernels, 4 * TILE, 2 * TILE), BF),
                pltpu.VMEM((visits, height, columns), F32),
                pltpu.VMEM((CHUNKS, n_list, crows, columns), F32),
                pltpu.VMEM((CHUNKS, n_list, crows, columns), F32),
                pltpu.VMEM((tall, columns), F32),
                pltpu.VMEM((height, columns), F32),
                pltpu.VMEM((n_band - 1, height, width), F32),
                pltpu.VMEM((n_sky * n_band, 8, TILE), F32),
                pltpu.VMEM((height, width), F32),
                dma((6,)), dma, dma, dma((2, visits)), dma((2, visits)), dma((CHUNKS,)), dma((CHUNKS,)),
                dma((2,)), dma((2,)), dma((n_sky * n_band - 1,)), dma((n_sky * n_band - 1,)), dma((n_band - 1,)), dma((n_band - 1,)), dma((2,)),
            ],
            compiler_params=pltpu.CompilerParams(
                collective_id=0, has_side_effects=True, vmem_limit_bytes=67043328
            ),
        )(images, valid_mask, jnp.swapaxes(row_kernel, 0, 1), jnp.swapaxes(col_kernel, 0, 1), psf_row, psf_col, exp_group, zero_point)

    placed = (
        P("band", "exp", ("patch", "sky"), None),
        P("band", "exp", ("patch", "sky"), None),
        P("band", "exp", None),
        P("band", "exp", None),
        P("band", "exp"),
        P("band", None),
        P("band", None),
        P("band", None),
    )
    return jax.shard_map(
        on_device,
        mesh=mesh,
        in_specs=placed,
        out_specs=(P("band", ("patch", "sky"), None), P(("patch", "sky"), "band")),
        check_vma=False,
    )
```

```python
import functools

import jax
import jax.numpy as jnp
from jax import lax
from jax.experimental import pallas as pl
from jax.experimental.pallas import tpu as pltpu
from jax.sharding import PartitionSpec as P

MESH = pl.DeviceIdType.MESH
HALF = 15
REJECT = 4
TAPS = 31
SENTINEL = 1e30
EPSILON = 1e-05
PAD = 16
TILE = 128
CHUNKS = 4
BF = jnp.bfloat16
F32 = jnp.float32


def parts(value):
    high = value.astype(BF)
    return high, (value - high.astype(F32)).astype(BF)


def mm(a, b):
    return jnp.dot(a, b, preferred_element_type=F32)


def cols_filter(high, low, wh_ref, wl_ref):
    columns = high.shape[1]
    outs = []
    for start in range(0, columns, 2 * TILE):
        lo_in, hi_in = max(start - TILE, 0), min(start + 3 * TILE, columns)
        base = lo_in - (start - TILE)
        span = pl.ds(base, hi_in - lo_in)
        wh, wl = wh_ref[span, :], wl_ref[span, :]
        h, l = high[:, lo_in:hi_in], low[:, lo_in:hi_in]
        outs.append(mm(h, wh) + mm(l, wh) + mm(h, wl))
    return outs


def insert(ordered, incoming, first, second):
    updated = []
    for held in ordered:
        updated.append(first(held, incoming))
        incoming = second(held, incoming)
    if len(updated) < REJECT:
        updated.append(incoming)
    return updated


def kernel(
    n_sky, n_band,
    img, mask, rk_in, ck_in, pr_in, pc_in, eg_in, zp_in,
    coadd_out, det_out,
    rk, ck, pr, pc, eg, zp, x, msk, taps_r, taps_c, trow, wh, wl, vals, lists, other, cpad, energy, peer_energy, sums, det,
    arg_sem, img_sem, mask_sem, halo_send, halo_recv, list_send, list_recv, share_send, share_recv, co_send, co_recv, sum_send, sum_recv,
    en_send, en_recv, out_sem,
):
    visits, height, columns = img.shape[1:]
    width = columns // n_band
    crows = height // CHUNKS
    sky, band, exp = lax.axis_index("sky"), lax.axis_index("band"), lax.axis_index("exp")
    has_before, has_after = sky > 0, sky < n_sky - 1
    n_peer = n_sky * n_band
    me = sky * n_band + band

    small = [
        pltpu.make_async_copy(source, target, arg_sem.at[k])
        for k, (source, target) in enumerate(
            ((eg_in, eg), (zp_in, zp), (ck_in, ck), (pc_in, pc), (rk_in, rk), (pr_in, pr))
        )
    ]
    for copy in small:
        copy.start()
    load_img = pltpu.make_async_copy(img.at[0], x.at[:, pl.ds(PAD, height), :], img_sem)
    load_img.start()
    load_mask = pltpu.make_async_copy(mask.at[0], msk, mask_sem)
    load_mask.start()

    def peer_of(step):
        peer = lax.rem(me + step, n_peer)
        return {"sky": peer // n_band, "band": lax.rem(peer, n_band)}

    barrier = pltpu.get_barrier_semaphore()
    for step in range(1, n_peer):
        pl.semaphore_signal(barrier, inc=1, device_id=peer_of(step), device_id_type=MESH)
    pl.semaphore_signal(barrier, inc=1, device_id={"exp": 1 - exp}, device_id_type=MESH)

    taps_r[...] = jnp.zeros_like(taps_r)
    taps_c[...] = jnp.zeros_like(taps_c)
    for copy in small:
        copy.wait()
    for v in range(visits):
        taps_r[v:v + 1, 0:TAPS] = rk[v]
    taps_r[visits:visits + 1, 0:TAPS] = pr[...]
    for v in range(visits):
        taps_c[v:v + 1, 0:TAPS] = ck[v] * zp[0, eg[0, v]]
    taps_c[visits:visits + 1, 0:TAPS] = pc[...]
    at_row = lax.broadcasted_iota(jnp.int32, (TILE, TILE), 0)
    at_col = lax.broadcasted_iota(jnp.int32, (TILE, TILE), 1)
    flip = (at_col == lax.rem(HALF - at_row + TILE, TILE)).astype(F32)
    taps_c[...] = jnp.dot(taps_c[...], flip, preferred_element_type=F32, precision=lax.Precision.HIGHEST)

    def build(v, carry):
        band_r = jnp.broadcast_to(taps_r[pl.ds(v, 1), :], (TILE, TILE))
        band_r = pltpu.roll(band_r, 1, 1, stride=1, stride_axis=0)
        high, low = parts(jnp.where(at_col >= at_row, band_r, 0.0))
        trow[v, 0:TILE, 0:TILE] = high
        trow[v, TILE:2 * TILE, 0:TILE] = low
        high, low = parts(jnp.where(at_col < at_row, band_r, 0.0))
        trow[v, 0:TILE, TILE:2 * TILE] = high
        trow[v, TILE:2 * TILE, TILE:2 * TILE] = low
        band_c = jnp.broadcast_to(taps_c[pl.ds(v, 1), :], (TILE, TILE))
        band_c = pltpu.roll(band_c, 0, 1, stride=1, stride_axis=0)
        before = at_row - at_col > TILE // 2
        after = at_col - at_row > TILE // 2
        zero = jnp.zeros((TILE, TILE), BF)
        for half, ref in enumerate((wh, wl)):
            b_prev = parts(jnp.where(before, band_c, 0.0))[half]
            b_next = parts(jnp.where(after, band_c, 0.0))[half]
            b_here = parts(jnp.where(before | after, 0.0, band_c))[half]
            for k, row in enumerate(((b_prev, zero), (b_here, b_prev), (b_next, b_here), (zero, b_next))):
                for n, block in enumerate(row):
                    ref[v, k * TILE:(k + 1) * TILE, n * TILE:(n + 1) * TILE] = block
        return carry

    lax.fori_loop(0, visits // 2, build, 0)
    pl.semaphore_wait(barrier, n_peer)

    def halo(v, side):
        start, land = ((height - PAD, 0), (0, PAD + height))[side]
        return pltpu.make_async_remote_copy(
            src_ref=img.at[0, v, pl.ds(start, PAD), :],
            dst_ref=x.at[v, pl.ds(land, PAD), :],
            send_sem=halo_send.at[side, v], recv_sem=halo_recv.at[side, v],
            device_id={"sky": lax.rem(sky + (1, n_sky - 1)[side], n_sky)}, device_id_type=MESH,
        )

    def start_halo(v, carry):
        @pl.when(has_after)
        def _():
            halo(v, 0).start()

        @pl.when(has_before)
        def _():
            halo(v, 1).start()
        return carry

    lax.fori_loop(0, visits, start_halo, 0)
    lax.fori_loop(visits // 2, visits + 1, build, 0)

    @pl.when(jnp.logical_not(has_before))
    def _():
        x[:, 0:PAD, :] = jnp.zeros((visits, PAD, columns), BF)
        cpad[0:PAD, :] = jnp.zeros((PAD, columns), F32)

    @pl.when(jnp.logical_not(has_after))
    def _():
        x[:, PAD + height:, :] = jnp.zeros((visits, PAD, columns), BF)
        cpad[PAD + height:, :] = jnp.zeros((PAD, columns), F32)

    load_img.wait()
    tall = height + 2 * PAD

    once = 2 - visits % 2

    def convolve(i, carry):
        @pl.when(has_before)
        def _():
            for u in range(once):
                halo(i * once + u, 0).wait_recv()

        @pl.when(has_after)
        def _():
            for u in range(once):
                halo(i * once + u, 1).wait_recv()
        smeared = [mm(trow[i * once + u, :, 0:tall], x[i * once + u]) for u in range(once)]
        for u in range(once):
            v = i * once + u
            high, low = parts(smeared[u][0:height] + smeared[u][height:])
            for n, block in enumerate(cols_filter(high, low, wh.at[v], wl.at[v])):
                vals[v, :, n * 2 * TILE:(n + 1) * 2 * TILE] = block
        return carry

    lax.fori_loop(0, visits // once, convolve, 0)
    load_mask.wait()

    half = CHUNKS // 2
    own_first = exp * half
    far_first = (1 - exp) * half

    def exchange(c):
        return pltpu.make_async_remote_copy(
            src_ref=lists.at[far_first + c], dst_ref=other.at[c], send_sem=list_send.at[c], recv_sem=list_recv.at[c],
            device_id={"exp": 1 - exp}, device_id_type=MESH,
        )

    def select(order, carry):
        c = lax.rem(far_first + order, CHUNKS)

        def group(g, inner):
            rows = pl.ds(pl.multiple_of(c * crows + g * 8, 8), 8)
            upper, lower, total, count = [], [], None, None
            for v in range(visits):
                value, used = vals[v, rows, :], msk[v, rows, :]
                live = used == 1
                upper = insert(upper, jnp.where(live, value, -SENTINEL), jnp.maximum, jnp.minimum)
                lower = insert(lower, jnp.where(live, value, SENTINEL), jnp.minimum, jnp.maximum)
                kept = jnp.where(live, value, 0.0)
                total = kept if total is None else total + kept
                count = used if count is None else count + used
            spot = pl.ds(pl.multiple_of(g * 8, 8), 8)
            for k, item in enumerate(upper + lower + [total, count.astype(F32)]):
                lists[c, k, spot, :] = item
            return inner

        lax.fori_loop(0, crows // 8, group, 0)

        @pl.when(order < half)
        def _():
            exchange(order).start()
        return carry

    lax.fori_loop(0, CHUNKS, select, 0)

    def share(first, j):
        rows = pl.ds(pl.multiple_of(PAD + (first + j) * crows, 8), crows)
        return pltpu.make_async_remote_copy(
            src_ref=cpad.at[rows, :], dst_ref=cpad.at[rows, :], send_sem=share_send.at[j], recv_sem=share_recv.at[j],
            device_id={"exp": 1 - exp}, device_id_type=MESH,
        )

    def merge(j, carry):
        exchange(j).wait_recv()
        c = own_first + j

        def group(g, inner):
            spot = pl.ds(pl.multiple_of(g * 8, 8), 8)
            own = [lists[c, k, spot, :] for k in range(2 * REJECT + 2)]
            far = [other[j, k, spot, :] for k in range(2 * REJECT + 2)]
            ends = [jnp.maximum(own[k], far[REJECT - 1 - k]) for k in range(REJECT)]
            ends += [jnp.minimum(own[REJECT + k], far[2 * REJECT - 1 - k]) for k in range(REJECT)]
            upper_sum = (ends[0] + ends[1]) + (ends[2] + ends[3])
            lower_sum = (ends[4] + ends[5]) + (ends[6] + ends[7])
            flux, count = own[8] + far[8], own[9] + far[9]
            rows = pl.ds(pl.multiple_of(PAD + c * crows + g * 8, 8), 8)
            cpad[rows, :] = (flux - upper_sum - lower_sum) / (count - 2 * REJECT)
            return inner

        lax.fori_loop(0, crows // 8, group, 0)
        share(own_first, j).start()
        return carry

    lax.fori_loop(0, half, merge, 0)
    for j in range(half):
        share(far_first, j).wait_recv()

    def co_halo(side):
        start, land = ((height, 0), (PAD, PAD + height))[side]
        return pltpu.make_async_remote_copy(
            src_ref=cpad.at[pl.ds(start, PAD), :], dst_ref=cpad.at[pl.ds(land, PAD), :],
            send_sem=co_send.at[side], recv_sem=co_recv.at[side],
            device_id={"sky": lax.rem(sky + (1, n_sky - 1)[side], n_sky)}, device_id_type=MESH,
        )

    store_coadd = pltpu.make_async_copy(cpad.at[pl.ds(PAD, height), :], coadd_out.at[0], out_sem.at[0])

    @pl.when(has_after)
    def _():
        co_halo(0).start()

    @pl.when(has_before)
    def _():
        co_halo(1).start()
    store_coadd.start()

    @pl.when(has_before)
    def _():
        co_halo(0).wait_recv()

    @pl.when(has_after)
    def _():
        co_halo(1).wait_recv()
    high, low = parts(cpad[...])
    both = mm(trow[visits, :, 0:tall], high)
    smeared = both[0:height] + both[height:] + mm(trow[visits, 0:height, 0:tall], low)
    high, low = parts(smeared)
    partial = jnp.zeros((8, TILE), F32)
    for n, block in enumerate(cols_filter(high, low, wh.at[visits], wl.at[visits])):
        squared = block * block
        energy[:, n * 2 * TILE:(n + 1) * 2 * TILE] = squared
        for r in range(0, height, 8):
            for q in range(0, 2 * TILE, TILE):
                partial = partial + squared[r:r + 8, q:q + TILE]
    sums[pl.ds(me, 1)] = partial[None]

    def send_sum(step):
        return pltpu.make_async_remote_copy(
            src_ref=sums.at[me], dst_ref=sums.at[me], send_sem=sum_send.at[step - 1], recv_sem=sum_recv.at[step - 1],
            device_id=peer_of(step), device_id_type=MESH,
        )

    def send_energy(step):
        target = lax.rem(band + step, n_band)
        return pltpu.make_async_remote_copy(
            src_ref=energy.at[:, pl.ds(pl.multiple_of(target * width, TILE), width)],
            dst_ref=peer_energy.at[step - 1],
            send_sem=en_send.at[step - 1], recv_sem=en_recv.at[step - 1],
            device_id={"band": target}, device_id_type=MESH,
        )

    for step in range(1, n_peer):
        send_sum(step).start()
    for step in range(1, n_band):
        send_energy(step).start()
    for step in range(1, n_peer):
        send_sum(step).wait_recv()

    pixels = height * n_sky * columns

    def inverse(source):
        total = sums[source]
        for s in range(1, n_sky):
            total = total + sums[source + s * n_band]
        return 1.0 / (jnp.sum(total, keepdims=True) / pixels + EPSILON)

    mine = pl.ds(pl.multiple_of(band * width, TILE), width)
    total = energy[:, mine] * inverse(band)
    for step in range(1, n_band):
        send_energy(step).wait_recv()
        total = total + peer_energy[step - 1] * inverse(lax.rem(band + n_band - step, n_band))
    det[...] = total
    store_det = pltpu.make_async_copy(det, det_out, out_sem.at[1])
    store_det.start()

    def drain(v, carry):
        @pl.when(has_after)
        def _():
            halo(v, 0).wait_send()

        @pl.when(has_before)
        def _():
            halo(v, 1).wait_send()
        return carry

    lax.fori_loop(0, visits, drain, 0)

    @pl.when(has_after)
    def _():
        co_halo(0).wait_send()

    @pl.when(has_before)
    def _():
        co_halo(1).wait_send()
    for j in range(half):
        exchange(j).wait_send()
        share(own_first, j).wait_send()
    for step in range(1, n_peer):
        send_sum(step).wait_send()
    for step in range(1, n_band):
        send_energy(step).wait_send()
    store_coadd.wait()
    store_det.wait()


def solution(mesh):
    n_sky, n_band = mesh.shape["sky"], mesh.shape["band"]

    def on_device(images, valid_mask, row_kernel, col_kernel, exp_group, zero_point, psf_row, psf_col):
        _, visits, height, columns = images.shape
        assert height == TILE and mesh.shape["exp"] == 2 and visits >= REJECT
        width = columns // n_band
        tall = height + 2 * PAD
        n_list = 2 * REJECT + 2
        crows = height // CHUNKS
        kernels = visits + 1
        table = -(-kernels // 8) * 8
        hbm, anywhere = (pl.BlockSpec(memory_space=space) for space in (pltpu.HBM, pl.ANY))
        dma = pltpu.SemaphoreType.DMA
        return pl.pallas_call(
            functools.partial(kernel, n_sky, n_band),
            out_shape=(
                jax.ShapeDtypeStruct((1, height, columns), F32),
                jax.ShapeDtypeStruct((height, width), F32),
            ),
            in_specs=[hbm] * 8,
            out_specs=(anywhere, anywhere),
            scratch_shapes=[
                pltpu.VMEM((visits, 1, TAPS), F32),
                pltpu.VMEM((visits, 1, TAPS), F32),
                pltpu.VMEM((1, TAPS), F32),
                pltpu.VMEM((1, TAPS), F32),
                pltpu.SMEM(exp_group.shape, jnp.int32),
                pltpu.SMEM(zero_point.shape, F32),
                pltpu.VMEM((visits, tall, columns), BF),
                pltpu.VMEM((visits, height, columns), jnp.int32),
                pltpu.VMEM((table, TILE), F32),
                pltpu.VMEM((table, TILE), F32),
                pltpu.VMEM((kernels, 2 * TILE, 2 * TILE), BF),
                pltpu.VMEM((kernels, 4 * TILE, 2 * TILE), BF),
                pltpu.VMEM((kernels, 4 * TILE, 2 * TILE), BF),
                pltpu.VMEM((visits, height, columns), F32),
                pltpu.VMEM((CHUNKS, n_list, crows, columns), F32),
                pltpu.VMEM((CHUNKS // 2, n_list, crows, columns), F32),
                pltpu.VMEM((tall, columns), F32),
                pltpu.VMEM((height, columns), F32),
                pltpu.VMEM((n_band - 1, height, width), F32),
                pltpu.VMEM((n_sky * n_band, 8, TILE), F32),
                pltpu.VMEM((height, width), F32),
                dma((6,)), dma, dma, dma((2, visits)), dma((2, visits)), dma((CHUNKS // 2,)), dma((CHUNKS // 2,)), dma((CHUNKS // 2,)), dma((CHUNKS // 2,)),
                dma((2,)), dma((2,)), dma((n_sky * n_band - 1,)), dma((n_sky * n_band - 1,)), dma((n_band - 1,)), dma((n_band - 1,)), dma((2,)),
            ],
            compiler_params=pltpu.CompilerParams(
                collective_id=0, has_side_effects=True, vmem_limit_bytes=66600000
            ),
        )(images, valid_mask, jnp.swapaxes(row_kernel, 0, 1), jnp.swapaxes(col_kernel, 0, 1), psf_row, psf_col, exp_group, zero_point)

    placed = (
        P("band", "exp", ("patch", "sky"), None),
        P("band", "exp", ("patch", "sky"), None),
        P("band", "exp", None),
        P("band", "exp", None),
        P("band", "exp"),
        P("band", None),
        P("band", None),
        P("band", None),
    )
    return jax.shard_map(
        on_device,
        mesh=mesh,
        in_specs=placed,
        out_specs=(P("band", ("patch", "sky"), None), P(("patch", "sky"), "band")),
        check_vma=False,
    )
```

```python
import functools

import jax
import jax.numpy as jnp
from jax import lax
from jax.experimental import pallas as pl
from jax.experimental.pallas import tpu as pltpu
from jax.sharding import PartitionSpec as P

MESH = pl.DeviceIdType.MESH
HALF = 15
REJECT = 4
TAPS = 31
SENTINEL = 1e30
EPSILON = 1e-05
PAD = 16
TILE = 128
CHUNKS = 4
BF = jnp.bfloat16
F32 = jnp.float32


def parts(value):
    high = value.astype(BF)
    return high, (value - high.astype(F32)).astype(BF)


def mm(a, b):
    return jnp.dot(a, b, preferred_element_type=F32)


def cols_filter(high, low, wh_ref, wl_ref):
    columns = high.shape[1]
    outs = []
    for start in range(0, columns, 2 * TILE):
        lo_in, hi_in = max(start - TILE, 0), min(start + 3 * TILE, columns)
        base = lo_in - (start - TILE)
        span = pl.ds(base, hi_in - lo_in)
        wh, wl = wh_ref[span, :], wl_ref[span, :]
        h, l = high[:, lo_in:hi_in], low[:, lo_in:hi_in]
        outs.append(mm(h, wh) + mm(l, wh) + mm(h, wl))
    return outs


def insert(ordered, incoming, first, second):
    updated = []
    for held in ordered:
        updated.append(first(held, incoming))
        incoming = second(held, incoming)
    if len(updated) < REJECT:
        updated.append(incoming)
    return updated


def kernel(
    n_sky, n_band,
    img, mask, rk_in, ck_in, pr_in, pc_in, eg_in, zp_in,
    coadd_out, det_out,
    rk, ck, pr, pc, eg, zp, x, msk, taps_r, taps_c, trow, wh, wl, vals, lists, other, cpad, energy, peer_energy, sums, det,
    arg_sem, img_sem, mask_sem, halo_send, halo_recv, list_send, list_recv, share_send, share_recv, co_send, co_recv, sum_send, sum_recv,
    en_send, en_recv, out_sem,
):
    visits, height, columns = img.shape[1:]
    width = columns // n_band
    crows = height // CHUNKS
    sky, band, exp = lax.axis_index("sky"), lax.axis_index("band"), lax.axis_index("exp")
    has_before, has_after = sky > 0, sky < n_sky - 1
    n_peer = n_sky * n_band
    me = sky * n_band + band

    small = [
        pltpu.make_async_copy(source, target, arg_sem.at[k])
        for k, (source, target) in enumerate(
            ((eg_in, eg), (zp_in, zp), (ck_in, ck), (pc_in, pc), (rk_in, rk), (pr_in, pr))
        )
    ]
    for copy in small:
        copy.start()
    load_img = pltpu.make_async_copy(img.at[0], x.at[:, pl.ds(PAD, height), :], img_sem)
    load_img.start()
    load_mask = pltpu.make_async_copy(mask.at[0], msk, mask_sem)
    load_mask.start()

    def peer_of(step):
        peer = lax.rem(me + step, n_peer)
        return {"sky": peer // n_band, "band": lax.rem(peer, n_band)}

    barrier = pltpu.get_barrier_semaphore()
    for step in range(1, n_peer):
        pl.semaphore_signal(barrier, inc=1, device_id=peer_of(step), device_id_type=MESH)
    pl.semaphore_signal(barrier, inc=1, device_id={"exp": 1 - exp}, device_id_type=MESH)

    taps_r[...] = jnp.zeros_like(taps_r)
    taps_c[...] = jnp.zeros_like(taps_c)
    for copy in small:
        copy.wait()
    for v in range(visits):
        taps_r[v:v + 1, 0:TAPS] = rk[v]
    taps_r[visits:visits + 1, 0:TAPS] = pr[...]
    for v in range(visits):
        taps_c[v:v + 1, 0:TAPS] = ck[v] * zp[0, eg[0, v]]
    taps_c[visits:visits + 1, 0:TAPS] = pc[...]
    at_row = lax.broadcasted_iota(jnp.int32, (TILE, TILE), 0)
    at_col = lax.broadcasted_iota(jnp.int32, (TILE, TILE), 1)
    flip = (at_col == lax.rem(HALF - at_row + TILE, TILE)).astype(F32)
    taps_c[...] = jnp.dot(taps_c[...], flip, preferred_element_type=F32, precision=lax.Precision.HIGHEST)

    def build(v, carry):
        band_r = jnp.broadcast_to(taps_r[pl.ds(v, 1), :], (TILE, TILE))
        band_r = pltpu.roll(band_r, 1, 1, stride=1, stride_axis=0)
        high, low = parts(jnp.where(at_col >= at_row, band_r, 0.0))
        trow[v, 0:TILE, 0:TILE] = high
        trow[v, TILE:2 * TILE, 0:TILE] = low
        high, low = parts(jnp.where(at_col < at_row, band_r, 0.0))
        trow[v, 0:TILE, TILE:2 * TILE] = high
        trow[v, TILE:2 * TILE, TILE:2 * TILE] = low
        band_c = jnp.broadcast_to(taps_c[pl.ds(v, 1), :], (TILE, TILE))
        band_c = pltpu.roll(band_c, 0, 1, stride=1, stride_axis=0)
        before = at_row - at_col > TILE // 2
        after = at_col - at_row > TILE // 2
        zero = jnp.zeros((TILE, TILE), BF)
        for half, ref in enumerate((wh, wl)):
            b_prev = parts(jnp.where(before, band_c, 0.0))[half]
            b_next = parts(jnp.where(after, band_c, 0.0))[half]
            b_here = parts(jnp.where(before | after, 0.0, band_c))[half]
            for k, row in enumerate(((b_prev, zero), (b_here, b_prev), (b_next, b_here), (zero, b_next))):
                for n, block in enumerate(row):
                    ref[v, k * TILE:(k + 1) * TILE, n * TILE:(n + 1) * TILE] = block
        return carry

    lax.fori_loop(0, visits // 2, build, 0)
    pl.semaphore_wait(barrier, n_peer)

    def halo(v, side):
        start, land = ((height - PAD, 0), (0, PAD + height))[side]
        return pltpu.make_async_remote_copy(
            src_ref=img.at[0, v, pl.ds(start, PAD), :],
            dst_ref=x.at[v, pl.ds(land, PAD), :],
            send_sem=halo_send.at[side, v], recv_sem=halo_recv.at[side, v],
            device_id={"sky": lax.rem(sky + (1, n_sky - 1)[side], n_sky)}, device_id_type=MESH,
        )

    def start_halo(v, carry):
        @pl.when(has_after)
        def _():
            halo(v, 0).start()

        @pl.when(has_before)
        def _():
            halo(v, 1).start()
        return carry

    lax.fori_loop(0, visits, start_halo, 0)
    lax.fori_loop(visits // 2, visits + 1, build, 0)

    @pl.when(jnp.logical_not(has_before))
    def _():
        x[:, 0:PAD, :] = jnp.zeros((visits, PAD, columns), BF)
        cpad[0:PAD, :] = jnp.zeros((PAD, columns), F32)

    @pl.when(jnp.logical_not(has_after))
    def _():
        x[:, PAD + height:, :] = jnp.zeros((visits, PAD, columns), BF)
        cpad[PAD + height:, :] = jnp.zeros((PAD, columns), F32)

    load_img.wait()
    tall = height + 2 * PAD

    once = next(u for u in (5, 2, 1) if visits % u == 0)

    def convolve(i, carry):
        @pl.when(has_before)
        def _():
            for u in range(once):
                halo(i * once + u, 0).wait_recv()

        @pl.when(has_after)
        def _():
            for u in range(once):
                halo(i * once + u, 1).wait_recv()
        smeared = [mm(trow[i * once + u, :, 0:tall], x[i * once + u]) for u in range(once)]
        for u in range(once):
            v = i * once + u
            high, low = parts(smeared[u][0:height] + smeared[u][height:])
            for n, block in enumerate(cols_filter(high, low, wh.at[v], wl.at[v])):
                vals[v, :, n * 2 * TILE:(n + 1) * 2 * TILE] = block
        return carry

    lax.fori_loop(0, visits // once, convolve, 0)
    load_mask.wait()

    half = CHUNKS // 2
    own_first = exp * half
    far_first = (1 - exp) * half

    def exchange(c):
        return pltpu.make_async_remote_copy(
            src_ref=lists.at[far_first + c], dst_ref=other.at[c], send_sem=list_send.at[c], recv_sem=list_recv.at[c],
            device_id={"exp": 1 - exp}, device_id_type=MESH,
        )

    def select(order, carry):
        c = lax.rem(far_first + order, CHUNKS)

        def group(g, inner):
            rows = pl.ds(pl.multiple_of(c * crows + g * 8, 8), 8)
            upper, lower, total, count = [], [], None, None
            for v in range(visits):
                value, used = vals[v, rows, :], msk[v, rows, :]
                live = used == 1
                upper = insert(upper, jnp.where(live, value, -SENTINEL), jnp.maximum, jnp.minimum)
                lower = insert(lower, jnp.where(live, value, SENTINEL), jnp.minimum, jnp.maximum)
                kept = jnp.where(live, value, 0.0)
                total = kept if total is None else total + kept
                count = used if count is None else count + used
            spot = pl.ds(pl.multiple_of(g * 8, 8), 8)
            for k, item in enumerate(upper + lower + [total, count.astype(F32)]):
                lists[c, k, spot, :] = item
            return inner

        lax.fori_loop(0, crows // 8, group, 0)

        @pl.when(order < half)
        def _():
            exchange(order).start()
        return carry

    lax.fori_loop(0, CHUNKS, select, 0)

    def share(first, j):
        rows = pl.ds(pl.multiple_of(PAD + (first + j) * crows, 8), crows)
        return pltpu.make_async_remote_copy(
            src_ref=cpad.at[rows, :], dst_ref=cpad.at[rows, :], send_sem=share_send.at[j], recv_sem=share_recv.at[j],
            device_id={"exp": 1 - exp}, device_id_type=MESH,
        )

    def merge(j, carry):
        exchange(j).wait_recv()
        c = own_first + j

        def group(g, inner):
            spot = pl.ds(pl.multiple_of(g * 8, 8), 8)
            own = [lists[c, k, spot, :] for k in range(2 * REJECT + 2)]
            far = [other[j, k, spot, :] for k in range(2 * REJECT + 2)]
            ends = [jnp.maximum(own[k], far[REJECT - 1 - k]) for k in range(REJECT)]
            ends += [jnp.minimum(own[REJECT + k], far[2 * REJECT - 1 - k]) for k in range(REJECT)]
            upper_sum = (ends[0] + ends[1]) + (ends[2] + ends[3])
            lower_sum = (ends[4] + ends[5]) + (ends[6] + ends[7])
            flux, count = own[8] + far[8], own[9] + far[9]
            rows = pl.ds(pl.multiple_of(PAD + c * crows + g * 8, 8), 8)
            cpad[rows, :] = (flux - upper_sum - lower_sum) / (count - 2 * REJECT)
            return inner

        lax.fori_loop(0, crows // 8, group, 0)
        share(own_first, j).start()
        return carry

    lax.fori_loop(0, half, merge, 0)
    for j in range(half):
        share(far_first, j).wait_recv()

    def co_halo(side):
        start, land = ((height, 0), (PAD, PAD + height))[side]
        return pltpu.make_async_remote_copy(
            src_ref=cpad.at[pl.ds(start, PAD), :], dst_ref=cpad.at[pl.ds(land, PAD), :],
            send_sem=co_send.at[side], recv_sem=co_recv.at[side],
            device_id={"sky": lax.rem(sky + (1, n_sky - 1)[side], n_sky)}, device_id_type=MESH,
        )

    store_coadd = pltpu.make_async_copy(cpad.at[pl.ds(PAD, height), :], coadd_out.at[0], out_sem.at[0])

    @pl.when(has_after)
    def _():
        co_halo(0).start()

    @pl.when(has_before)
    def _():
        co_halo(1).start()
    store_coadd.start()

    @pl.when(has_before)
    def _():
        co_halo(0).wait_recv()

    @pl.when(has_after)
    def _():
        co_halo(1).wait_recv()
    high, low = parts(cpad[...])
    both = mm(trow[visits, :, 0:tall], high)
    smeared = both[0:height] + both[height:] + mm(trow[visits, 0:height, 0:tall], low)
    high, low = parts(smeared)
    partial = jnp.zeros((8, TILE), F32)
    for n, block in enumerate(cols_filter(high, low, wh.at[visits], wl.at[visits])):
        squared = block * block
        energy[:, n * 2 * TILE:(n + 1) * 2 * TILE] = squared
        for r in range(0, height, 8):
            for q in range(0, 2 * TILE, TILE):
                partial = partial + squared[r:r + 8, q:q + TILE]
    sums[pl.ds(me, 1)] = partial[None]

    def send_sum(step):
        return pltpu.make_async_remote_copy(
            src_ref=sums.at[me], dst_ref=sums.at[me], send_sem=sum_send.at[step - 1], recv_sem=sum_recv.at[step - 1],
            device_id=peer_of(step), device_id_type=MESH,
        )

    def send_energy(step):
        target = lax.rem(band + step, n_band)
        return pltpu.make_async_remote_copy(
            src_ref=energy.at[:, pl.ds(pl.multiple_of(target * width, TILE), width)],
            dst_ref=peer_energy.at[step - 1],
            send_sem=en_send.at[step - 1], recv_sem=en_recv.at[step - 1],
            device_id={"band": target}, device_id_type=MESH,
        )

    for step in range(1, n_peer):
        send_sum(step).start()
    for step in range(1, n_band):
        send_energy(step).start()
    for step in range(1, n_peer):
        send_sum(step).wait_recv()

    pixels = height * n_sky * columns

    def inverse(source):
        total = sums[source]
        for s in range(1, n_sky):
            total = total + sums[source + s * n_band]
        return 1.0 / (jnp.sum(total, keepdims=True) / pixels + EPSILON)

    mine = pl.ds(pl.multiple_of(band * width, TILE), width)
    total = energy[:, mine] * inverse(band)
    for step in range(1, n_band):
        send_energy(step).wait_recv()
        total = total + peer_energy[step - 1] * inverse(lax.rem(band + n_band - step, n_band))
    det[...] = total
    store_det = pltpu.make_async_copy(det, det_out, out_sem.at[1])
    store_det.start()

    def drain(v, carry):
        @pl.when(has_after)
        def _():
            halo(v, 0).wait_send()

        @pl.when(has_before)
        def _():
            halo(v, 1).wait_send()
        return carry

    lax.fori_loop(0, visits, drain, 0)

    @pl.when(has_after)
    def _():
        co_halo(0).wait_send()

    @pl.when(has_before)
    def _():
        co_halo(1).wait_send()
    for j in range(half):
        exchange(j).wait_send()
        share(own_first, j).wait_send()
    for step in range(1, n_peer):
        send_sum(step).wait_send()
    for step in range(1, n_band):
        send_energy(step).wait_send()
    store_coadd.wait()
    store_det.wait()


def solution(mesh):
    n_sky, n_band = mesh.shape["sky"], mesh.shape["band"]

    def on_device(images, valid_mask, row_kernel, col_kernel, exp_group, zero_point, psf_row, psf_col):
        _, visits, height, columns = images.shape
        assert height == TILE and mesh.shape["exp"] == 2 and visits >= REJECT
        width = columns // n_band
        tall = height + 2 * PAD
        n_list = 2 * REJECT + 2
        crows = height // CHUNKS
        kernels = visits + 1
        table = -(-kernels // 8) * 8
        hbm, anywhere = (pl.BlockSpec(memory_space=space) for space in (pltpu.HBM, pl.ANY))
        dma = pltpu.SemaphoreType.DMA
        return pl.pallas_call(
            functools.partial(kernel, n_sky, n_band),
            out_shape=(
                jax.ShapeDtypeStruct((1, height, columns), F32),
                jax.ShapeDtypeStruct((height, width), F32),
            ),
            in_specs=[hbm] * 8,
            out_specs=(anywhere, anywhere),
            scratch_shapes=[
                pltpu.VMEM((visits, 1, TAPS), F32),
                pltpu.VMEM((visits, 1, TAPS), F32),
                pltpu.VMEM((1, TAPS), F32),
                pltpu.VMEM((1, TAPS), F32),
                pltpu.SMEM(exp_group.shape, jnp.int32),
                pltpu.SMEM(zero_point.shape, F32),
                pltpu.VMEM((visits, tall, columns), BF),
                pltpu.VMEM((visits, height, columns), jnp.int32),
                pltpu.VMEM((table, TILE), F32),
                pltpu.VMEM((table, TILE), F32),
                pltpu.VMEM((kernels, 2 * TILE, 2 * TILE), BF),
                pltpu.VMEM((kernels, 4 * TILE, 2 * TILE), BF),
                pltpu.VMEM((kernels, 4 * TILE, 2 * TILE), BF),
                pltpu.VMEM((visits, height, columns), F32),
                pltpu.VMEM((CHUNKS, n_list, crows, columns), F32),
                pltpu.VMEM((CHUNKS // 2, n_list, crows, columns), F32),
                pltpu.VMEM((tall, columns), F32),
                pltpu.VMEM((height, columns), F32),
                pltpu.VMEM((n_band - 1, height, width), F32),
                pltpu.VMEM((n_sky * n_band, 8, TILE), F32),
                pltpu.VMEM((height, width), F32),
                dma((6,)), dma, dma, dma((2, visits)), dma((2, visits)), dma((CHUNKS // 2,)), dma((CHUNKS // 2,)), dma((CHUNKS // 2,)), dma((CHUNKS // 2,)),
                dma((2,)), dma((2,)), dma((n_sky * n_band - 1,)), dma((n_sky * n_band - 1,)), dma((n_band - 1,)), dma((n_band - 1,)), dma((2,)),
            ],
            compiler_params=pltpu.CompilerParams(
                collective_id=0, has_side_effects=True, vmem_limit_bytes=66600000
            ),
        )(images, valid_mask, jnp.swapaxes(row_kernel, 0, 1), jnp.swapaxes(col_kernel, 0, 1), psf_row, psf_col, exp_group, zero_point)

    placed = (
        P("band", "exp", ("patch", "sky"), None),
        P("band", "exp", ("patch", "sky"), None),
        P("band", "exp", None),
        P("band", "exp", None),
        P("band", "exp"),
        P("band", None),
        P("band", None),
        P("band", None),
    )
    return jax.shard_map(
        on_device,
        mesh=mesh,
        in_specs=placed,
        out_specs=(P("band", ("patch", "sky"), None), P(("patch", "sky"), "band")),
        check_vma=False,
    )
```
